32 devices in a mesh: seq: 2 (over x), tensor: 16 (over z, y, core).
Axes of the slice: x: 2, y: 2, z: 4, core: 2. Of those that a mesh axis runs over, the one named last changes fastest.
Arguments:
- tokens: bfloat16 [512, 4096], P(('seq', 'tensor')), may hold values from -6 to 6
- lengths: int32 [6], replicated, may hold values from 1 to 256, 512 in all
- proj_zx: bfloat16 [4096, 2, 8192], P(None, None, 'tensor'), may hold values from -0.09375 to 0.09375
- proj_bc: bfloat16 [4096, 2, 1024], P(None, None, 'tensor'), may hold values from -0.09375 to 0.09375
- proj_dt: bfloat16 [4096, 128], P(None, 'tensor'), may hold values from -0.09375 to 0.09375
- conv_x: float32 [4, 8192], P(None, 'tensor'), may hold values from -3 to 3
- conv_bc: float32 [4, 2, 1024], P(None, None, 'tensor'), may hold values from -3 to 3
- bias_x: float32 [8192], P('tensor'), may hold values from -0.5 to 0.5
- bias_bc: float32 [2, 1024], P(None, 'tensor'), may hold values from -0.5 to 0.5
- dt_bias: float32 [128], P('tensor'), may hold values from -7 to -3
- decay_rate: float32 [128], P('tensor'), may hold values from 0.02 to 1
- skip_gain: float32 [128], P('tensor'), may hold values from 0.5 to 1.5
- proj_out: bfloat16 [8192, 4096], P('tensor'), may hold values from -0.0625 to 0.0625
Outputs:
- mixed: bfloat16 [512, 4096], P(('seq', 'tensor'))
- final_states: float32 [6, 128, 64, 128], P(None, 'tensor')
The draws below stay inside these ranges and needn't reach their ends.
Inputs may be any that keep to these rules, and one draw needn't show every extreme that they name: `lengths`: the 6 requests lie back to back in the stream in this order and fill it exactly; the longest has exactly 256 tokens.
All inputs are finite; a program needn't handle non-finite values.
Results may differ from the reference program's by a relative error of at most 0.0074.
Values may be sent and summed in bfloat16 or wider, within the bound.
A program may use at most 128 MiB of HBM per device.

```python
import math
import jax
import jax.numpy as jnp
import numpy as np
from jax import lax

D = 4096
HEADS = 128
HEAD = 64
GROUPS = 8
STATE = 128
KCONV = 4
INNER = 8192
NSEG = 6
TOKENS = 512


def levels(own_key, shape, split, low, top_value):
    factor_of = 1.0
    for position, parts in split:
        draws = jax.random.uniform(jax.random.fold_in(jax.random.fold_in(own_key, 6), position), (parts,), jnp.float32, low / len(split), top_value / len(split))
        factor_of = factor_of * jnp.repeat(jnp.exp(draws), shape[position] // parts).reshape((-1,) + (1,) * (len(shape) - 1 - position))
    return factor_of


def profile(amount, total, reach, slope):
    loads = [(1 << 20) // math.isqrt(grade ** slope) + 1 for grade in range(2, amount + 1)]
    surplus, holding = total - reach - (amount - 1), [1] * (amount - 1)
    while surplus > 0:
        movable = [i for i in range(amount - 1) if holding[i] < reach]
        mass, remaining = sum([loads[i] for i in movable]), surplus
        for i in movable:
            extra = min(reach - holding[i], max(1, remaining * loads[i] // mass), surplus)
            holding[i] = holding[i] + extra
            surplus = surplus - extra
    return np.array([reach] + holding)


def ragged_sizes(rng, amount, total, reach, lean):
    if amount == 2:
        one = jax.random.randint(rng, (), max(1, total - reach), min(reach, total - 1) + 1)
        return jnp.stack([one, total - one])
    sizes = jnp.asarray(profile(amount, total, reach, lean), jnp.int32)
    twos = (amount - 1) // 2
    source_of, taker = sizes[1:1 + 2 * twos:2], sizes[2:2 + 2 * twos:2]
    slack = jnp.minimum(source_of - 1, reach - taker)
    moved = jax.random.randint(jax.random.fold_in(rng, 1), (twos,), 0, 1 << 20) % (slack + 1)
    sizes = sizes.at[1:1 + 2 * twos:2].set(source_of - moved).at[2:2 + 2 * twos:2].set(taker + moved)
    return sizes[jax.random.permutation(jax.random.fold_in(rng, 2), amount)]


def normal_values(own_key, shape, width, most, cuts=(), held_as=jnp.bfloat16):
    entries = jax.random.normal(own_key, shape, jnp.float32) * width
    if len(cuts) > 0:
        entries = levels(own_key, shape, cuts, -0.22, 0.18) * entries
    return jnp.clip(entries, min=-most, max=most).astype(held_as)


def setup_inputs(seed: int = 0) -> dict:
    splits = jax.random.split(jax.random.key(seed), 14)
    tokens = normal_values(splits[0], (TOKENS, D), 1.0, 6.0, ((0, 32),))
    lengths = ragged_sizes(splits[1], NSEG, TOKENS, TOKENS // 2, 2).astype(jnp.int32)
    proj_zx = normal_values(splits[2], (D, 2, INNER), D ** -0.5, 0.09375, ((2, 16),))
    proj_bc = normal_values(splits[3], (D, 2, GROUPS * STATE), D ** -0.5, 0.09375, ((2, 16),))
    proj_dt = normal_values(splits[4], (D, HEADS), D ** -0.5, 0.09375, ((1, 16),))
    conv_x = normal_values(splits[5], (KCONV, INNER), KCONV ** -0.5, 3.0, ((1, 16),), jnp.float32)
    conv_bc = normal_values(splits[6], (KCONV, 2, GROUPS * STATE), KCONV ** -0.5, 3.0, ((2, 16),), jnp.float32)
    bias_x = jnp.clip(jax.random.uniform(splits[7], (INNER,), jnp.float32, -0.5, 0.5) * levels(splits[7], (INNER,), ((0, 16),), -0.4, 0.0), -0.5, 0.5)
    bias_bc = jnp.clip(jax.random.uniform(splits[8], (2, GROUPS * STATE), jnp.float32, -0.5, 0.5) * levels(splits[8], (2, GROUPS * STATE), ((1, 16),), -0.4, 0.0), -0.5, 0.5)
    dt_bias = jnp.clip(-7.0 + 4.0 * jax.random.uniform(splits[9], (HEADS,), jnp.float32) ** levels(splits[9], (HEADS,), ((0, 16),), -0.2, 0.2), -7.0, -3.0)
    decay_rate = jnp.clip(jnp.exp(math.log(1.0) - 3.912023 * jax.random.uniform(splits[10], (HEADS,), jnp.float32) ** levels(splits[10], (HEADS,), ((0, 16),), -0.2, 0.2)), 0.02, 1.0)
    skip_gain = jnp.clip(0.5 + 1.0 * jax.random.uniform(splits[11], (HEADS,), jnp.float32) ** levels(splits[11], (HEADS,), ((0, 16),), -0.2, 0.2), 0.5, 1.5)
    proj_out = normal_values(splits[12], (INNER, D), INNER ** -0.5, 0.0625, ((0, 16),))
    return {"tokens": tokens, "lengths": lengths, "proj_zx": proj_zx, "proj_bc": proj_bc, "proj_dt": proj_dt, "conv_x": conv_x, "conv_bc": conv_bc, "bias_x": bias_x, "bias_bc": bias_bc, "dt_bias": dt_bias, "decay_rate": decay_rate, "skip_gain": skip_gain, "proj_out": proj_out}


def conv_segment(pre_conv, taps, offset, positions, seg_start):
    values = pre_conv.astype(jnp.float32)
    count = values.shape[0]
    result = jnp.zeros_like(values) + offset[None, :]
    for lag_index in range(taps.shape[0]):
        shifted = jnp.pad(values, ((lag_index, 0), (0, 0)))[:count]
        keep_mask = (positions - lag_index >= seg_start).astype(jnp.float32)
        result = result + taps[lag_index][None, :] * shifted * keep_mask[:, None]
    return result


def reference(tokens, lengths, proj_zx, proj_bc, proj_dt, conv_x, conv_bc, bias_x, bias_bc, dt_bias, decay_rate, skip_gain, proj_out):
    total = tokens.shape[0]
    zx_all = jnp.dot(tokens, proj_zx.reshape(D, 2 * INNER), preferred_element_type=jnp.float32)
    gate_in = zx_all[:, :INNER].astype(jnp.bfloat16)
    x_in = zx_all[:, INNER:].astype(jnp.bfloat16)
    bc_in = jnp.dot(tokens, proj_bc.reshape(D, 2 * GROUPS * STATE), preferred_element_type=jnp.float32).astype(jnp.bfloat16)
    step_size = jax.nn.softplus(jnp.dot(tokens, proj_dt, preferred_element_type=jnp.float32) + dt_bias[None, :])
    positions = jnp.arange(total, dtype=jnp.int32)
    bounds = jnp.cumsum(lengths).astype(jnp.int32)
    reached = bounds[None, :] <= positions[:, None]
    segment = jnp.sum(reached.astype(jnp.int32), axis=1).astype(jnp.int32)
    seg_start = jnp.max(jnp.where(reached, bounds[None, :], 0), axis=1).astype(jnp.int32)
    x_conv = jax.nn.silu(conv_segment(x_in, conv_x, bias_x, positions, seg_start)).astype(jnp.bfloat16)
    bc_conv = jax.nn.silu(conv_segment(bc_in, conv_bc.reshape(KCONV, 2 * GROUPS * STATE), bias_bc.reshape(2 * GROUPS * STATE), positions, seg_start)).astype(jnp.bfloat16)
    bc_float = bc_conv.astype(jnp.float32).reshape(total, 2, GROUPS, STATE)
    x_heads = x_conv.astype(jnp.float32).reshape(total, HEADS, HEAD)
    per_group = HEADS // GROUPS
    is_start = positions == seg_start
    last_pos = jnp.take(bounds, segment) - 1
    is_end = positions == last_pos

    def advance(carry, item):
        state, finals = carry
        step_now, x_now, b_now, c_now, start_now, end_now, seg_now = item
        keep = jnp.where(start_now, 0.0, 1.0).astype(jnp.float32)
        decay = jnp.exp(-decay_rate * step_now) * keep
        b_rep = jnp.repeat(b_now, per_group, axis=0)
        c_rep = jnp.repeat(c_now, per_group, axis=0)
        state = state * decay[:, None, None] + (step_now[:, None] * x_now)[:, :, None] * b_rep[:, None, :]
        y_now = jnp.einsum('hpn,hn->hp', state, c_rep, precision=lax.Precision.HIGHEST) + skip_gain[:, None] * x_now
        current = lax.dynamic_index_in_dim(finals, seg_now, 0, keepdims=False)
        finals = lax.dynamic_update_index_in_dim(finals, jnp.where(end_now, state, current), seg_now, 0)
        return (state, finals), y_now

    init = (jnp.zeros((HEADS, HEAD, STATE), jnp.float32), jnp.zeros((NSEG, HEADS, HEAD, STATE), jnp.float32))
    items = (step_size, x_heads, bc_float[:, 0], bc_float[:, 1], is_start, is_end, segment)
    (state_last, final_states), y_all = lax.scan(advance, init, items)
    gate_values = jax.nn.silu(gate_in.astype(jnp.float32)).reshape(total, HEADS, HEAD)
    gated = (y_all * gate_values).reshape(total, INNER).astype(jnp.bfloat16)
    mixed = jnp.dot(gated, proj_out, preferred_element_type=jnp.float32).astype(jnp.bfloat16)
    return mixed, final_states
```

```python
import jax
import jax.numpy as jnp
from jax import lax
from jax.experimental import pallas as pl
from jax.experimental.pallas import tpu as pltpu
from jax.sharding import PartitionSpec as P

GROUPS = 8


def partner_2(value, axis, bit):
    mask = 2**bit
    pairs = [(source, source ^ mask) for source in range(lax.axis_size(axis))]
    return lax.ppermute(value, axis, pairs)


def passed_along(block, axis, distance):
    devices = range(lax.axis_size(axis))
    route = [(i - distance, i) for i in devices if i - distance in devices]
    return lax.ppermute(block, axis, route)


def group_columns(bc_own, tensor_index, steps_count):
    collected = bc_own
    for bit_number in range(steps_count):
        partner = partner_2(collected, "tensor", bit_number)
        upper = tensor_index // 2**bit_number % 2
        low_first = jnp.concatenate([collected, partner], axis=2)
        high_first = jnp.concatenate([partner, collected], axis=2)
        collected = jnp.where(upper == 0, low_first, high_first)
    return collected


def body(
    tokens,
    lengths,
    proj_zx,
    proj_bc,
    proj_dt,
    conv_x,
    conv_bc,
    bias_x,
    bias_bc,
    dt_bias,
    decay_rate,
    skip_gain,
    proj_out,
):
    highest = lax.Precision.HIGHEST
    tensor_size = lax.axis_size("tensor")
    rows_dev = tokens.shape[0]
    shard_len = rows_dev * tensor_size
    seq_index = lax.axis_index("seq")
    tensor_index = lax.axis_index("tensor")
    heads_dev = decay_rate.shape[0]
    width_zx = proj_zx.shape[2]
    head_size = width_zx // heads_dev
    cols_bc = proj_bc.shape[2]
    taps_count = conv_x.shape[0]
    model_width = tokens.shape[1]
    zx_flat = proj_zx.reshape(model_width, 2 * width_zx)
    bc_flat = proj_bc.reshape(model_width, 2 * cols_bc)
    piece = lax.all_gather(tokens, "tensor", axis=0, tiled=True)
    projected = jnp.concatenate(
        [
            jnp.dot(piece, zx_flat, preferred_element_type=jnp.float32),
            jnp.dot(piece, bc_flat, preferred_element_type=jnp.float32),
            jnp.dot(piece, proj_dt, preferred_element_type=jnp.float32),
        ],
        axis=1,
    )
    gate_in = projected[:, :width_zx].astype(jnp.bfloat16)
    conv_in = projected[:, width_zx : 2 * width_zx + 2 * cols_bc].astype(jnp.bfloat16)
    step_size = jax.nn.softplus(projected[:, 2 * width_zx + 2 * cols_bc :] + dt_bias[None, :])
    row_ids = jnp.arange(shard_len, dtype=jnp.int32)
    positions = seq_index * shard_len + row_ids
    bounds = jnp.cumsum(lengths)
    reached = bounds[None, :] <= positions[:, None]
    segment = jnp.sum(reached.astype(jnp.int32), axis=1)
    seg_start = jnp.max(jnp.where(reached, bounds[None, :], 0), axis=1)
    edge_rows = conv_in[shard_len - (taps_count - 1) :]
    before = passed_along(edge_rows, "seq", 1)
    extended = jnp.concatenate([before, conv_in], axis=0)
    conv_taps = jnp.concatenate([conv_x, conv_bc.reshape(taps_count, 2 * cols_bc)], axis=1)
    conv_offset = jnp.concatenate([bias_x, bias_bc.reshape(2 * cols_bc)])
    convolved = jnp.zeros((shard_len, conv_taps.shape[1]), jnp.float32) + conv_offset[None, :]
    for lag_index in range(taps_count):
        lagged = extended[
            taps_count - 1 - lag_index : taps_count - 1 - lag_index + shard_len
        ].astype(jnp.float32)
        keep_mask = (positions - lag_index >= seg_start).astype(jnp.float32)
        convolved = convolved + conv_taps[lag_index][None, :] * lagged * keep_mask[:, None]
    activated = jax.nn.silu(convolved).astype(jnp.bfloat16)
    x_conv = activated[:, :width_zx]
    bc_own = activated[:, width_zx:].reshape(shard_len, 2, cols_bc)
    per_group = tensor_size // GROUPS
    steps_count = per_group.bit_length() - 1
    bc_group = group_columns(bc_own, tensor_index, steps_count).astype(jnp.float32)
    state_in_proj = bc_group[:, 0]
    state_out_proj = bc_group[:, 1]
    x_float = x_conv.astype(jnp.float32).reshape(shard_len, heads_dev, head_size)
    log_decay = -decay_rate[None, :] * step_size
    cumulative = jnp.cumsum(log_decay, axis=0)
    cumulative_t = cumulative.T
    valid = (segment[:, None] == segment[None, :]) & (row_ids[:, None] >= row_ids[None, :])
    spread = cumulative_t[:, :, None] - cumulative_t[:, None, :]
    decay_matrix = jnp.where(valid[None], jnp.exp(jnp.where(valid[None], spread, 0.0)), 0.0)
    scores = jnp.dot(state_out_proj, state_in_proj.T, precision=highest)
    mixing = decay_matrix * scores[None] * step_size.T[:, None, :]
    y_local = jnp.einsum("hts,shp->thp", mixing, x_float, precision=highest)
    before_pos = seq_index * shard_len - 1
    seg_before = jnp.sum((bounds <= before_pos).astype(jnp.int32))
    carried = (segment == seg_before).astype(jnp.float32)
    entry_gain = jnp.exp(cumulative) * carried[:, None]
    n_seg = lengths.shape[0]
    end_rows = bounds - 1 - seq_index * shard_len
    inside = (end_rows >= 0) & (end_rows < shard_len)
    target_rows = jnp.concatenate([end_rows, jnp.full((1,), shard_len - 1, jnp.int32)])
    target_seg = jnp.concatenate([jnp.arange(n_seg, dtype=jnp.int32), segment[shard_len - 1 :]])
    target_ok = jnp.concatenate([inside, jnp.ones((1,), bool)])
    picker = (row_ids[None, :] == target_rows[:, None]).astype(jnp.float32)
    cum_end = jnp.dot(picker, cumulative, precision=highest)
    reach = (
        target_ok[:, None]
        & (row_ids[None, :] <= target_rows[:, None])
        & (segment[None, :] == target_seg[:, None])
    )
    gap_end = cum_end[:, :, None] - cumulative_t[None, :, :]
    end_weight = (
        jnp.where(reach[:, None, :], jnp.exp(jnp.where(reach[:, None, :], gap_end, 0.0)), 0.0)
        * step_size.T[None]
    )
    states = jnp.einsum("khs,shp,sn->khpn", end_weight, x_float, state_in_proj, precision=highest)
    end_local = states[:n_seg]
    shard_state = states[n_seg]
    end_gain = jnp.where((target_ok & (target_seg == seg_before))[:, None], jnp.exp(cum_end), 0.0)
    shard_gain = end_gain[n_seg]
    end_gain_seg = end_gain[:n_seg]
    gathered = (
        lax.all_gather(shard_gain[None], "seq", axis=0, tiled=True),
        lax.all_gather(shard_state[None], "seq", axis=0, tiled=True),
        lax.all_gather(end_gain_seg[None], "seq", axis=0, tiled=True),
        lax.all_gather(end_local[None], "seq", axis=0, tiled=True),
    )
    gains_all, states_all, egains_all, elocal_all = gathered

    def fold_step(carry, item):
        gain_now, state_now = item
        return (gain_now[:, None, None] * carry + state_now, carry)

    last_state, incoming = lax.scan(
        fold_step, jnp.zeros(shard_state.shape, jnp.float32), (gains_all, states_all)
    )
    state_entry = lax.dynamic_index_in_dim(incoming, seq_index, 0, keepdims=False)
    final_states = jnp.sum(elocal_all + egains_all[:, :, :, None, None] * incoming[:, None], axis=0)
    y_entry = (
        jnp.einsum("tn,hpn->thp", state_out_proj, state_entry, precision=highest)
        * entry_gain[:, :, None]
    )
    y_total = y_local + y_entry + skip_gain[None, :, None] * x_float
    gate_values = jax.nn.silu(gate_in.astype(jnp.float32)).reshape(shard_len, heads_dev, head_size)
    gated = (y_total * gate_values).reshape(shard_len, width_zx).astype(jnp.bfloat16)
    mixed = lax.psum_scatter(
        jnp.dot(gated, proj_out, preferred_element_type=jnp.float32),
        "tensor",
        scatter_dimension=0,
        tiled=True,
    )
    return (mixed.astype(jnp.bfloat16), final_states)


F32 = jnp.float32
BF16 = jnp.bfloat16
ROWS = 16
LEN = 256
WIDE = 4096
CHAN = 512
STATES = 128
HIGH = lax.Precision.HIGHEST
NT = (((1,), (1,)), ((), ()))
TN = (((0,), (0,)), ((), ()))


def remote(src, dst, send, recv, **device):
    return pltpu.make_async_remote_copy(
        src_ref=src,
        dst_ref=dst,
        send_sem=send,
        recv_sem=recv,
        device_id=device,
        device_id_type=pl.DeviceIdType.MESH,
    )


def segment_of(bounds, pos):
    total = jnp.zeros(pos.shape, jnp.int32)
    for bound in bounds:
        total = total + (bound <= pos).astype(jnp.int32)
    return total


def layer_kernel(
    lengths,
    tok_in,
    zx_in,
    bc_in,
    dt_in,
    taps_x,
    taps_bc,
    dt_bias,
    rate,
    skip,
    out_in,
    mixed,
    finals,
    tok,
    zx_raw,
    w_zx,
    w_bc,
    w_out,
    t_bc,
    gate,
    ext,
    act,
    steps,
    fin,
    acc,
    keep,
    send_a,
    recv_a,
    send_b,
    recv_b,
    send_c,
    recv_c,
    load_sem,
    zx_sem,
    agz_s,
    agz_r,
    agy_s,
    agy_r,
    agc_s,
    agc_r,
    misc_s,
    misc_r,
    rsa_s,
    rsa_r,
    rsb_s,
    rsb_r,
    rsc_s,
    rsc_r,
):
    s = lax.axis_index("seq")
    me = lax.axis_index("tensor")
    z = me // 4
    y = (me // 2) % 2
    c = me % 2
    oy = 1 - y
    oc = 1 - c
    sib = z * 4 + y * 2 + oc
    ypal = z * 4 + oy * 2 + c
    zpal = [((z + d) % 4) * 4 + y * 2 + c for d in range(4)]
    other = 1 - s

    own = pltpu.make_async_copy(tok_in, tok.at[z, y, c], load_sem.at[0])
    own.start()
    zx_loads = []
    for i in range(4):
        rows = pl.ds(i * 1024, 1024)
        load = pltpu.make_async_copy(zx_in.at[rows], zx_raw.at[rows], zx_sem.at[i])
        load.start()
        zx_loads.append(load)
    bc_load = pltpu.make_async_copy(bc_in, w_bc.at[:, c], load_sem.at[1])
    bc_load.start()
    tap_load = pltpu.make_async_copy(taps_bc, t_bc.at[c], load_sem.at[2])
    tap_load.start()
    out_load = pltpu.make_async_copy(out_in, w_out, load_sem.at[3])
    out_load.start()

    barrier = pltpu.get_barrier_semaphore()
    for pal in [sib, ypal] + zpal[1:]:
        pl.semaphore_signal(
            barrier, inc=1, device_id={"tensor": pal}, device_id_type=pl.DeviceIdType.MESH
        )
    pl.semaphore_signal(
        barrier, inc=1, device_id={"seq": other}, device_id_type=pl.DeviceIdType.MESH
    )
    pl.semaphore_wait(barrier, 6)

    started = []

    def go(copy):
        copy.start()
        started.append(copy)
        return copy

    def block(d, yy, cc):
        return tok.at[(z + 4 - d) % 4, yy, cc]

    here = tok.at[z, y, c]
    ysend = [go(remote(tok_in, here, agy_s.at[0], agy_r.at[0], tensor=ypal))]
    zsend = [None]
    for d in (1, 2, 3):
        zsend.append(go(remote(tok_in, here, agz_s.at[d], agz_r.at[d], tensor=zpal[d])))
    csend = {0: go(remote(tok_in, here, agc_s.at[0], agc_r.at[0], tensor=sib))}
    bc_send = go(remote(bc_in, w_bc.at[:, c], misc_s.at[0], misc_r.at[0], tensor=sib))
    tap_send = go(remote(taps_bc, t_bc.at[c], misc_s.at[1], misc_r.at[1], tensor=sib))

    def split(i):
        zx_loads[i].wait()

        @pl.loop(0, 8)
        def _(j):
            rows = pl.ds(pl.multiple_of(i * 1024 + j * 128, 128), 128)
            pair = pltpu.einshape("abc->bac", zx_raw[rows])
            w_zx[rows, :CHAN] = pair[0]
            w_zx[rows, CHAN:] = pair[1]

    for d in (1, 3, 2):
        zsend[d].wait_recv()
        mine = block(d, y, c)
        go(remote(mine, mine, agy_s.at[d], agy_r.at[d], tensor=ypal))
        go(remote(mine, mine, agc_s.at[d], agc_r.at[d], tensor=sib))
        if d != 2:
            split(0 if d == 1 else 1)
    for d in (0, 1, 3, 2):
        theirs = block(d, oy, c)
        remote(theirs, theirs, agy_s.at[d], agy_r.at[d], tensor=ypal).wait_recv()
        go(remote(theirs, theirs, agc_s.at[4 + d], agc_r.at[4 + d], tensor=sib))
        if d == 0:
            split(2)
        if d == 1:
            split(3)
    own.wait()
    bc_load.wait()
    tap_load.wait()
    bc_send.wait_recv()
    tap_send.wait_recv()
    for d in range(4):
        for k, yy in ((0, y), (4, oy)):
            blk = block(d, yy, oc)
            remote(blk, blk, agc_s.at[k + d], agc_r.at[k + d], tensor=sib).wait_recv()

    def stream():
        return tok[...].reshape(LEN, WIDE)

    for i in range(2):
        cols = slice(CHAN + i * 256, CHAN + i * 256 + 256)
        ext[16:, i * 256 : i * 256 + 256] = jnp.dot(
            stream(), w_zx[:, cols], preferred_element_type=F32
        ).astype(BF16)
    ext[16:, CHAN:] = lax.dot_general(
        stream(), w_bc[...].reshape(256, WIDE), NT, preferred_element_type=F32
    ).astype(BF16)
    halo = go(
        remote(ext.at[pl.ds(256, 16)], ext.at[pl.ds(0, 16)], misc_s.at[2], misc_r.at[2], seq=other)
    )
    dt_raw = lax.dot_general(dt_in[...], stream(), NT, preferred_element_type=F32)
    dt_raw = dt_raw + dt_bias[...]
    steps[s] = jax.nn.softplus(dt_raw)
    step_send = go(remote(steps.at[s], steps.at[s], misc_s.at[3], misc_r.at[3], seq=other))
    for i in range(2):
        cols = slice(i * 256, i * 256 + 256)
        gate[:, cols] = jnp.dot(stream(), w_zx[:, cols], preferred_element_type=F32).astype(BF16)

    n_seg = lengths.shape[0]
    bounds = []
    run = jnp.int32(0)
    for k in range(n_seg):
        run = run + lengths[k]
        bounds.append(run)
    base = s * LEN
    pos = lax.broadcasted_iota(jnp.int32, (LEN, 128), 0) + base
    seg_start = jnp.zeros((LEN, 128), jnp.int32)
    for bound in bounds:
        seg_start = jnp.where(bound <= pos, jnp.maximum(seg_start, bound), seg_start)
    masks = [(pos - j >= seg_start).astype(F32) for j in range(4)]

    halo.wait_recv()

    def taps_for(i, row):
        if i < 4:
            return taps_x[row : row + 1, i * 128 : i * 128 + 128]
        lo = (i - 4) * 64
        return jnp.concatenate(
            [t_bc[0, row : row + 1, lo : lo + 64], t_bc[1, row : row + 1, lo : lo + 64]], axis=1
        )

    for i in range(6):
        cols = slice(i * 128, i * 128 + 128)
        v = ext[:, cols].astype(F32)
        total = jnp.zeros((LEN, 128), F32) + taps_for(i, 4)
        for j in range(4):
            lagged = v if j == 0 else pltpu.roll(v, j, 0)
            total = total + taps_for(i, j) * lagged[16:] * masks[j]
        act[s, :, cols] = (total * lax.logistic(total)).astype(BF16)
    act_send = go(
        remote(
            act.at[s, :, pl.ds(0, 640)],
            act.at[s, :, pl.ds(0, 640)],
            misc_s.at[4],
            misc_r.at[4],
            seq=other,
        )
    )

    ri = lax.broadcasted_iota(jnp.int32, (LEN, LEN), 0)
    ci = lax.broadcasted_iota(jnp.int32, (LEN, LEN), 1)
    upper = (ri <= ci).astype(F32)
    head_of = lax.broadcasted_iota(jnp.int32, (8, CHAN), 1) // 64
    spread = (head_of == lax.broadcasted_iota(jnp.int32, (8, CHAN), 0)).astype(F32)

    def cumulate(dt):
        return jnp.dot(-rate[...] * dt, upper, precision=HIGH, preferred_element_type=F32)

    def widen(rows):
        return lax.dot_general(rows, spread, TN, precision=HIGH, preferred_element_type=F32)

    dt_own = steps[s]
    cum_r = cumulate(dt_own)
    cum_c = cum_r.T
    seg_r = segment_of(bounds, ci + base)
    seg_c = segment_of(bounds, ri + base)
    valid = (seg_r == seg_c) & (ri >= ci)
    b_own = act[s, :, CHAN : CHAN + STATES]
    c_own = act[s, :, CHAN + STATES :]
    scores = lax.dot_general(c_own, b_own, NT, preferred_element_type=F32)
    scores = jnp.where(valid, scores, 0.0)
    lane = lax.broadcasted_iota(jnp.int32, (LEN, 128), 1)
    for g in range(4):
        cols = slice(g * 128, g * 128 + 128)
        x_pair = act[s, :, cols]
        halves = []
        for h in (2 * g, 2 * g + 1):
            gap = cum_c[:, h : h + 1] - cum_r[h : h + 1, :]
            mix = jnp.exp(jnp.where(valid, gap, 0.0)) * scores * dt_own[h : h + 1, :]
            halves.append(jnp.dot(mix.astype(BF16), x_pair, preferred_element_type=F32))
        acc[:, cols] = jnp.where(lane < 64, halves[0], halves[1])

    step_send.wait_recv()
    act_send.wait_recv()
    dt_0 = steps[0]
    cum_0 = cumulate(dt_0)
    end_0 = jnp.sum(-rate[...] * dt_0, axis=1, keepdims=True)
    seg_before = segment_of(bounds, jnp.full((8, LEN), LEN - 1, jnp.int32))
    place = lax.broadcasted_iota(jnp.int32, (8, LEN), 1)
    seg_0 = segment_of(bounds, place)
    seg_1 = segment_of(bounds, place + LEN)
    seg_own = segment_of(bounds, place + base)
    last_0 = cum_0[:, LEN - 1 :]
    into = jnp.exp(last_0 - cum_0) * dt_0 * (seg_0 == seg_before).astype(F32)
    x_0 = act[0, :, :CHAN].astype(F32)
    x_in = (x_0 * widen(into)).astype(BF16)
    entry = lax.dot_general(
        act[0, :, CHAN : CHAN + STATES], x_in, TN, preferred_element_type=F32
    ).astype(BF16)
    carried = ((seg_own == seg_before) & (s > 0)).astype(F32)
    gain = widen(jnp.exp(cum_r) * carried)
    y_all = acc[:, :CHAN] + jnp.dot(c_own, entry, preferred_element_type=F32) * gain
    y_all = y_all + skip[...] * act[s, :, :CHAN].astype(F32)
    gate_f = gate[...].astype(F32)
    gate[...] = (y_all * (gate_f * lax.logistic(gate_f))).astype(BF16)
    out_load.wait()

    @pl.loop(0, 8)
    def _(i):
        cols = pl.ds(pl.multiple_of(i * 512, 512), 512)
        acc[:, cols] = jnp.dot(gate[...], w_out[:, cols], preferred_element_type=F32)

    def part(d, yy, cc):
        return pl.ds(pl.multiple_of(((z + d) % 4) * 64 + yy * 32 + cc * 16, 16), 16)

    order = (2, 1, 3, 0)
    a_copy = {}
    for d in order:
        for yy in range(2):
            send_a[d, yy] = acc[part(d, yy, oc), :].astype(BF16)
        a_copy[d] = go(
            remote(send_a.at[d], recv_a.at[d], rsa_s.at[d], rsa_r.at[d], tensor=sib)
        )
    b_copy = {}
    for d in order:
        a_copy[d].wait_recv()
        send_b[d] = (acc[part(d, oy, c), :] + recv_a[d, oy].astype(F32)).astype(BF16)
        b_copy[d] = go(
            remote(send_b.at[d], recv_b.at[d], rsb_s.at[d], rsb_r.at[d], tensor=ypal)
        )
        keep[d] = acc[part(d, y, c), :] + recv_a[d, y].astype(F32)

    def finals_part():
        dt_1 = steps[1]
        cum_1 = cumulate(dt_1) + last_0
        ends_0 = jnp.zeros((8, LEN), F32)
        ends_1 = jnp.zeros((8, LEN), F32)
        for k in range(n_seg):
            spot_0 = (place == bounds[k] - 1).astype(F32) * cum_0
            spot_1 = (place + LEN == bounds[k] - 1).astype(F32) * cum_1
            end = jnp.sum(spot_0 + spot_1, axis=1, keepdims=True)
            ends_0 = jnp.where(seg_0 == k, end, ends_0)
            ends_1 = jnp.where(seg_1 == k, end, ends_1)
        w_0 = widen(jnp.exp(ends_0 - cum_0) * dt_0)
        w_1 = widen(jnp.exp(ends_1 - cum_1) * dt_1)
        x_1 = act[1, :, :CHAN].astype(F32)
        xw_0 = (x_0 * w_0).astype(BF16)
        xw_1 = (x_1 * w_1).astype(BF16)
        b_0 = act[0, :, CHAN : CHAN + STATES]
        b_1 = act[1, :, CHAN : CHAN + STATES]
        spot = lax.broadcasted_iota(jnp.int32, (LEN, STATES), 0)
        col_0 = segment_of(bounds, spot)
        col_1 = segment_of(bounds, spot + LEN)
        for k in range(n_seg):
            m_0 = jnp.where(col_0 == k, b_0.astype(F32), 0.0).astype(BF16)
            m_1 = jnp.where(col_1 == k, b_1.astype(F32), 0.0).astype(BF16)
            fin[k] = lax.dot_general(
                xw_0, m_0, TN, preferred_element_type=F32
            ) + lax.dot_general(xw_1, m_1, TN, preferred_element_type=F32)

    c_copy = {}
    for d in order:
        b_copy[d].wait_recv()
        summed = keep[d] + recv_b[d].astype(F32)
        if d == 0:
            keep[0] = summed
        else:
            send_c[d] = summed.astype(BF16)
            c_copy[d] = go(
                remote(send_c.at[d], recv_c.at[d], rsc_s.at[d], rsc_r.at[d], tensor=zpal[d])
            )
        if d == 2:
            finals_part()
            fin_out = pltpu.make_async_copy(fin, finals, load_sem.at[4])
            fin_out.start()
    total = keep[0]
    for d in (1, 3, 2):
        c_copy[d].wait_recv()
        total = total + recv_c[d].astype(F32)
    mixed[...] = total.astype(BF16)
    for copy in started:
        copy.wait_send()
    fin_out.wait()


def fused_body(
    tokens,
    lengths,
    proj_zx,
    proj_bc,
    proj_dt,
    conv_x,
    conv_bc,
    bias_x,
    bias_bc,
    dt_bias,
    decay_rate,
    skip_gain,
    proj_out,
):
    n_seg = lengths.shape[0]
    bc_view = proj_bc.transpose(1, 2, 0)
    dt_view = proj_dt.T
    taps_x = jnp.concatenate([conv_x, bias_x[None], jnp.zeros((3, CHAN), F32)], axis=0)
    taps_bc = jnp.concatenate(
        [conv_bc.reshape(4, 128), bias_bc.reshape(1, 128), jnp.zeros((3, 128), F32)], axis=0
    )
    any_spec = pl.BlockSpec(memory_space=pl.ANY)
    vmem = pl.BlockSpec(memory_space=pltpu.VMEM)
    dma = pltpu.SemaphoreType.DMA
    mixed, finals = pl.pallas_call(
        layer_kernel,
        out_shape=(
            jax.ShapeDtypeStruct((ROWS, WIDE), BF16),
            jax.ShapeDtypeStruct((n_seg, CHAN, STATES), F32),
        ),
        in_specs=[pl.BlockSpec(memory_space=pltpu.SMEM), any_spec, any_spec, any_spec]
        + [vmem, vmem, any_spec, vmem, vmem, vmem, any_spec],
        out_specs=(vmem, any_spec),
        scratch_shapes=[
            pltpu.VMEM((4, 2, 2, ROWS, WIDE), BF16),
            pltpu.VMEM((WIDE, 2, CHAN), BF16),
            pltpu.VMEM((WIDE, 2 * CHAN), BF16),
            pltpu.VMEM((2, 2, 64, WIDE), BF16),
            pltpu.VMEM((CHAN, WIDE), BF16),
            pltpu.VMEM((2, 8, 128), F32),
            pltpu.VMEM((LEN, CHAN), BF16),
            pltpu.VMEM((16 + LEN, CHAN + 256), BF16),
            pltpu.VMEM((2, LEN, CHAN + 256), BF16),
            pltpu.VMEM((2, 8, LEN), F32),
            pltpu.VMEM((n_seg, CHAN, STATES), F32),
            pltpu.VMEM((LEN, WIDE), F32),
            pltpu.VMEM((4, ROWS, WIDE), F32),
            pltpu.VMEM((4, 2, ROWS, WIDE), BF16),
            pltpu.VMEM((4, 2, ROWS, WIDE), BF16),
            pltpu.VMEM((4, ROWS, WIDE), BF16),
            pltpu.VMEM((4, ROWS, WIDE), BF16),
            pltpu.VMEM((4, ROWS, WIDE), BF16),
            pltpu.VMEM((4, ROWS, WIDE), BF16),
            dma((5,)),
            dma((4,)),
            dma((4,)),
            dma((4,)),
            dma((4,)),
            dma((4,)),
            dma((8,)),
            dma((8,)),
            dma((5,)),
            dma((5,)),
            dma((4,)),
            dma((4,)),
            dma((4,)),
            dma((4,)),
            dma((4,)),
            dma((4,)),
        ],
        compiler_params=pltpu.CompilerParams(
            collective_id=0, has_side_effects=True, vmem_limit_bytes=60 << 20
        ),
    )(
        lengths,
        tokens,
        proj_zx,
        bc_view,
        dt_view,
        taps_x,
        taps_bc,
        dt_bias.reshape(8, 1),
        decay_rate.reshape(8, 1),
        jnp.repeat(skip_gain, 64).reshape(1, CHAN),
        proj_out,
    )
    return (mixed, finals.reshape(n_seg, 8, 64, STATES))


def solution(mesh):
    in_specs = (
        P(("seq", "tensor"), None),
        P(),
        P(None, None, "tensor"),
        P(None, None, "tensor"),
        P(None, "tensor"),
        P(None, "tensor"),
        P(None, None, "tensor"),
        P("tensor"),
        P(None, "tensor"),
        P("tensor"),
        P("tensor"),
        P("tensor"),
        P("tensor", None),
    )
    out_specs = (P(("seq", "tensor"), None), P(None, "tensor", None, None))
    small = mesh.shape["seq"] == 2 and mesh.shape["tensor"] == 16
    chosen = fused_body if small else body
    return jax.shard_map(chosen, mesh=mesh, in_specs=in_specs, out_specs=out_specs, check_vma=False)
```

```python
import jax
import jax.numpy as jnp
from jax import lax
from jax.experimental import pallas as pl
from jax.experimental.pallas import tpu as pltpu
from jax.sharding import PartitionSpec as P

GROUPS = 8


def partner_2(value, axis, bit):
    mask = 2**bit
    pairs = [(source, source ^ mask) for source in range(lax.axis_size(axis))]
    return lax.ppermute(value, axis, pairs)


def passed_along(block, axis, distance):
    devices = range(lax.axis_size(axis))
    route = [(i - distance, i) for i in devices if i - distance in devices]
    return lax.ppermute(block, axis, route)


def group_columns(bc_own, tensor_index, steps_count):
    collected = bc_own
    for bit_number in range(steps_count):
        partner = partner_2(collected, "tensor", bit_number)
        upper = tensor_index // 2**bit_number % 2
        low_first = jnp.concatenate([collected, partner], axis=2)
        high_first = jnp.concatenate([partner, collected], axis=2)
        collected = jnp.where(upper == 0, low_first, high_first)
    return collected


def body(
    tokens,
    lengths,
    proj_zx,
    proj_bc,
    proj_dt,
    conv_x,
    conv_bc,
    bias_x,
    bias_bc,
    dt_bias,
    decay_rate,
    skip_gain,
    proj_out,
):
    highest = lax.Precision.HIGHEST
    tensor_size = lax.axis_size("tensor")
    rows_dev = tokens.shape[0]
    shard_len = rows_dev * tensor_size
    seq_index = lax.axis_index("seq")
    tensor_index = lax.axis_index("tensor")
    heads_dev = decay_rate.shape[0]
    width_zx = proj_zx.shape[2]
    head_size = width_zx // heads_dev
    cols_bc = proj_bc.shape[2]
    taps_count = conv_x.shape[0]
    model_width = tokens.shape[1]
    zx_flat = proj_zx.reshape(model_width, 2 * width_zx)
    bc_flat = proj_bc.reshape(model_width, 2 * cols_bc)
    piece = lax.all_gather(tokens, "tensor", axis=0, tiled=True)
    projected = jnp.concatenate(
        [
            jnp.dot(piece, zx_flat, preferred_element_type=jnp.float32),
            jnp.dot(piece, bc_flat, preferred_element_type=jnp.float32),
            jnp.dot(piece, proj_dt, preferred_element_type=jnp.float32),
        ],
        axis=1,
    )
    gate_in = projected[:, :width_zx].astype(jnp.bfloat16)
    conv_in = projected[:, width_zx : 2 * width_zx + 2 * cols_bc].astype(jnp.bfloat16)
    step_size = jax.nn.softplus(projected[:, 2 * width_zx + 2 * cols_bc :] + dt_bias[None, :])
    row_ids = jnp.arange(shard_len, dtype=jnp.int32)
    positions = seq_index * shard_len + row_ids
    bounds = jnp.cumsum(lengths)
    reached = bounds[None, :] <= positions[:, None]
    segment = jnp.sum(reached.astype(jnp.int32), axis=1)
    seg_start = jnp.max(jnp.where(reached, bounds[None, :], 0), axis=1)
    edge_rows = conv_in[shard_len - (taps_count - 1) :]
    before = passed_along(edge_rows, "seq", 1)
    extended = jnp.concatenate([before, conv_in], axis=0)
    conv_taps = jnp.concatenate([conv_x, conv_bc.reshape(taps_count, 2 * cols_bc)], axis=1)
    conv_offset = jnp.concatenate([bias_x, bias_bc.reshape(2 * cols_bc)])
    convolved = jnp.zeros((shard_len, conv_taps.shape[1]), jnp.float32) + conv_offset[None, :]
    for lag_index in range(taps_count):
        lagged = extended[
            taps_count - 1 - lag_index : taps_count - 1 - lag_index + shard_len
        ].astype(jnp.float32)
        keep_mask = (positions - lag_index >= seg_start).astype(jnp.float32)
        convolved = convolved + conv_taps[lag_index][None, :] * lagged * keep_mask[:, None]
    activated = jax.nn.silu(convolved).astype(jnp.bfloat16)
    x_conv = activated[:, :width_zx]
    bc_own = activated[:, width_zx:].reshape(shard_len, 2, cols_bc)
    per_group = tensor_size // GROUPS
    steps_count = per_group.bit_length() - 1
    bc_group = group_columns(bc_own, tensor_index, steps_count).astype(jnp.float32)
    state_in_proj = bc_group[:, 0]
    state_out_proj = bc_group[:, 1]
    x_float = x_conv.astype(jnp.float32).reshape(shard_len, heads_dev, head_size)
    log_decay = -decay_rate[None, :] * step_size
    cumulative = jnp.cumsum(log_decay, axis=0)
    cumulative_t = cumulative.T
    valid = (segment[:, None] == segment[None, :]) & (row_ids[:, None] >= row_ids[None, :])
    spread = cumulative_t[:, :, None] - cumulative_t[:, None, :]
    decay_matrix = jnp.where(valid[None], jnp.exp(jnp.where(valid[None], spread, 0.0)), 0.0)
    scores = jnp.dot(state_out_proj, state_in_proj.T, precision=highest)
    mixing = decay_matrix * scores[None] * step_size.T[:, None, :]
    y_local = jnp.einsum("hts,shp->thp", mixing, x_float, precision=highest)
    before_pos = seq_index * shard_len - 1
    seg_before = jnp.sum((bounds <= before_pos).astype(jnp.int32))
    carried = (segment == seg_before).astype(jnp.float32)
    entry_gain = jnp.exp(cumulative) * carried[:, None]
    n_seg = lengths.shape[0]
    end_rows = bounds - 1 - seq_index * shard_len
    inside = (end_rows >= 0) & (end_rows < shard_len)
    target_rows = jnp.concatenate([end_rows, jnp.full((1,), shard_len - 1, jnp.int32)])
    target_seg = jnp.concatenate([jnp.arange(n_seg, dtype=jnp.int32), segment[shard_len - 1 :]])
    target_ok = jnp.concatenate([inside, jnp.ones((1,), bool)])
    picker = (row_ids[None, :] == target_rows[:, None]).astype(jnp.float32)
    cum_end = jnp.dot(picker, cumulative, precision=highest)
    reach = (
        target_ok[:, None]
        & (row_ids[None, :] <= target_rows[:, None])
        & (segment[None, :] == target_seg[:, None])
    )
    gap_end = cum_end[:, :, None] - cumulative_t[None, :, :]
    end_weight = (
        jnp.where(reach[:, None, :], jnp.exp(jnp.where(reach[:, None, :], gap_end, 0.0)), 0.0)
        * step_size.T[None]
    )
    states = jnp.einsum("khs,shp,sn->khpn", end_weight, x_float, state_in_proj, precision=highest)
    end_local = states[:n_seg]
    shard_state = states[n_seg]
    end_gain = jnp.where((target_ok & (target_seg == seg_before))[:, None], jnp.exp(cum_end), 0.0)
    shard_gain = end_gain[n_seg]
    end_gain_seg = end_gain[:n_seg]
    gathered = (
        lax.all_gather(shard_gain[None], "seq", axis=0, tiled=True),
        lax.all_gather(shard_state[None], "seq", axis=0, tiled=True),
        lax.all_gather(end_gain_seg[None], "seq", axis=0, tiled=True),
        lax.all_gather(end_local[None], "seq", axis=0, tiled=True),
    )
    gains_all, states_all, egains_all, elocal_all = gathered

    def fold_step(carry, item):
        gain_now, state_now = item
        return (gain_now[:, None, None] * carry + state_now, carry)

    last_state, incoming = lax.scan(
        fold_step, jnp.zeros(shard_state.shape, jnp.float32), (gains_all, states_all)
    )
    state_entry = lax.dynamic_index_in_dim(incoming, seq_index, 0, keepdims=False)
    final_states = jnp.sum(elocal_all + egains_all[:, :, :, None, None] * incoming[:, None], axis=0)
    y_entry = (
        jnp.einsum("tn,hpn->thp", state_out_proj, state_entry, precision=highest)
        * entry_gain[:, :, None]
    )
    y_total = y_local + y_entry + skip_gain[None, :, None] * x_float
    gate_values = jax.nn.silu(gate_in.astype(jnp.float32)).reshape(shard_len, heads_dev, head_size)
    gated = (y_total * gate_values).reshape(shard_len, width_zx).astype(jnp.bfloat16)
    mixed = lax.psum_scatter(
        jnp.dot(gated, proj_out, preferred_element_type=jnp.float32),
        "tensor",
        scatter_dimension=0,
        tiled=True,
    )
    return (mixed.astype(jnp.bfloat16), final_states)


F32 = jnp.float32
BF16 = jnp.bfloat16
ROWS = 16
LEN = 256
WIDE = 4096
CHAN = 512
STATES = 128
HIGH = lax.Precision.HIGHEST
NT = (((1,), (1,)), ((), ()))
TN = (((0,), (0,)), ((), ()))


def remote(src, dst, send, recv, **device):
    return pltpu.make_async_remote_copy(
        src_ref=src,
        dst_ref=dst,
        send_sem=send,
        recv_sem=recv,
        device_id=device,
        device_id_type=pl.DeviceIdType.MESH,
    )


def segment_of(bounds, pos):
    total = jnp.zeros(pos.shape, jnp.int32)
    for bound in bounds:
        total = total + (bound <= pos).astype(jnp.int32)
    return total


def layer_kernel(
    lengths,
    tok_in,
    zx_in,
    bc_in,
    dt_in,
    conv_x,
    bias_x,
    conv_bc,
    bias_bc,
    dt_bias,
    rate_in,
    skip_in,
    out_in,
    mixed,
    finals,
    tok,
    zx_raw,
    w_zx,
    w_bc,
    w_out,
    t_conv,
    t_bias,
    gate,
    ext,
    act,
    steps,
    fin,
    acc,
    keep,
    send_a,
    recv_a,
    send_b,
    recv_b,
    send_c,
    recv_c,
    load_sem,
    zx_sem,
    up_s,
    up_r,
    down_s,
    down_r,
    agy_s,
    agy_r,
    agc_s,
    agc_r,
    misc_s,
    misc_r,
    act_s,
    act_r,
    rsa_s,
    rsa_r,
    rsb_s,
    rsb_r,
    rsc_s,
    rsc_r,
):
    s = lax.axis_index("seq")
    me = lax.axis_index("tensor")
    z = me // 4
    y = (me // 2) % 2
    c = me % 2
    oy = 1 - y
    oc = 1 - c
    sib = z * 4 + y * 2 + oc
    ypal = z * 4 + oy * 2 + c
    zpal = [((z + d) % 4) * 4 + y * 2 + c for d in range(4)]
    other = 1 - s

    own = pltpu.make_async_copy(tok_in, tok.at[z, y, c], load_sem.at[0])
    own.start()
    zx_loads = []
    for i in range(4):
        rows = pl.ds(i * 1024, 1024)
        load = pltpu.make_async_copy(zx_in.at[rows], zx_raw.at[rows], zx_sem.at[i])
        load.start()
        zx_loads.append(load)
    bc_load = pltpu.make_async_copy(bc_in, w_bc.at[:, c], load_sem.at[1])
    bc_load.start()
    tap_load = pltpu.make_async_copy(conv_bc, t_conv.at[c], load_sem.at[2])
    tap_load.start()
    off_load = pltpu.make_async_copy(bias_bc, t_bias.at[c], load_sem.at[5])
    off_load.start()
    out_load = pltpu.make_async_copy(out_in, w_out, load_sem.at[3])
    out_load.start()

    barrier = pltpu.get_barrier_semaphore()
    for pal in [sib, ypal] + zpal[1:]:
        pl.semaphore_signal(
            barrier, inc=1, device_id={"tensor": pal}, device_id_type=pl.DeviceIdType.MESH
        )
    pl.semaphore_signal(
        barrier, inc=1, device_id={"seq": other}, device_id_type=pl.DeviceIdType.MESH
    )
    pl.semaphore_wait(barrier, 6)

    started = []

    def go(copy):
        copy.start()
        started.append(copy)
        return copy

    def block(zz, yy, cc):
        return tok.at[(zz + 4) % 4, yy, cc]

    guarded = []

    def maybe(condition, copy):
        pl.when(condition)(copy.start)
        guarded.append((condition, copy))

    here = tok.at[z, y, c]
    above = zpal[1]
    below = zpal[3]
    maybe(z < 3, remote(tok_in, here, up_s.at[0], up_r.at[1], tensor=above))
    maybe(z > 0, remote(tok_in, here, down_s.at[0], down_r.at[1], tensor=below))
    go(remote(tok_in, here, agy_s.at[z], agy_r.at[z], tensor=ypal))
    go(remote(tok_in, here, agc_s.at[z], agc_r.at[z], tensor=sib))
    bc_send = go(remote(bc_in, w_bc.at[:, c], misc_s.at[0], misc_r.at[0], tensor=sib))
    tap_send = go(remote(conv_bc, t_conv.at[c], misc_s.at[1], misc_r.at[1], tensor=sib))
    off_send = go(remote(bias_bc, t_bias.at[c], misc_s.at[5], misc_r.at[5], tensor=sib))

    def split(i):
        zx_loads[i].wait()

        @pl.loop(0, 8)
        def _(j):
            rows = pl.ds(pl.multiple_of(i * 1024 + j * 128, 128), 128)
            pair = pltpu.einshape("abc->bac", zx_raw[rows])
            w_zx[rows, :CHAN] = pair[0]
            w_zx[rows, CHAN:] = pair[1]

    def relay(k, zz, have, ahead, more, sends, recvs):
        mine = block(zz, y, c)
        at = (zz + 4) % 4

        @pl.when(have)
        def _():
            remote(mine, mine, sends.at[0], recvs.at[k], tensor=ahead).wait_recv()

        if k < 3:
            maybe(
                have & more, remote(mine, mine, sends.at[k], recvs.at[k + 1], tensor=ahead)
            )
        maybe(have, remote(mine, mine, agy_s.at[at], agy_r.at[at], tensor=ypal))
        maybe(have, remote(mine, mine, agc_s.at[at], agc_r.at[at], tensor=sib))

    def across(zz, have):
        theirs = block(zz, oy, c)
        at = (zz + 4) % 4

        @pl.when(have)
        def _():
            remote(theirs, theirs, agy_s.at[at], agy_r.at[at], tensor=ypal).wait_recv()

        maybe(
            have, remote(theirs, theirs, agc_s.at[4 + at], agc_r.at[4 + at], tensor=sib)
        )

    always = z >= 0
    split(0)
    for k in (1, 2, 3):
        relay(k, z - k, z >= k, above, z < 3, up_s, up_r)
        relay(k, z + k, z + k <= 3, below, z > 0, down_s, down_r)
        if k == 1:
            across(z, always)
        else:
            across(z - k + 1, z >= k - 1)
            across(z + k - 1, z + k - 1 <= 3)
        split(k)
    across(z - 3, z >= 3)
    across(z + 3, z + 3 <= 3)
    own.wait()
    for load in (bc_load, tap_load, off_load):
        load.wait()
    for sent in (bc_send, tap_send, off_send):
        sent.wait_recv()
    for d in range(4):
        for k, yy in ((0, y), (4, oy)):
            blk = tok.at[d, yy, oc]
            remote(blk, blk, agc_s.at[k + d], agc_r.at[k + d], tensor=sib).wait_recv()

    def stream():
        return tok[...].reshape(LEN, WIDE)

    for i in range(2):
        cols = slice(CHAN + i * 256, CHAN + i * 256 + 256)
        ext[16:, i * 256 : i * 256 + 256] = jnp.dot(
            stream(), w_zx[:, cols], preferred_element_type=F32
        ).astype(BF16)
    ext[16:, CHAN:] = lax.dot_general(
        stream(), w_bc[...].reshape(256, WIDE), NT, preferred_element_type=F32
    ).astype(BF16)
    halo = go(
        remote(ext.at[pl.ds(256, 16)], ext.at[pl.ds(0, 16)], misc_s.at[2], misc_r.at[2], seq=other)
    )
    dt_raw = lax.dot_general(dt_in[...], stream(), NT, preferred_element_type=F32)
    head_row = lax.broadcasted_iota(jnp.int32, (8, LEN), 0)

    def by_head(ref, heads):
        values = jnp.zeros(heads.shape, F32)
        for h in range(8):
            values = jnp.where(heads == h, ref[h], values)
        return values

    dt_raw = dt_raw + by_head(dt_bias, head_row)
    rate = by_head(rate_in, head_row)
    steps[s] = jax.nn.softplus(dt_raw)
    step_send = go(remote(steps.at[s], steps.at[s], misc_s.at[3], misc_r.at[3], seq=other))
    n_seg = lengths.shape[0]
    bounds = []
    run = jnp.int32(0)
    for k in range(n_seg):
        run = run + lengths[k]
        bounds.append(run)
    base = s * LEN
    pos = lax.broadcasted_iota(jnp.int32, (LEN, 128), 0) + base
    seg_start = jnp.zeros((LEN, 128), jnp.int32)
    for bound in bounds:
        seg_start = jnp.where(bound <= pos, jnp.maximum(seg_start, bound), seg_start)
    masks = [(pos - j >= seg_start).astype(F32) for j in range(4)]

    halo.wait_recv()

    def taps_for(i, row):
        if i < 4:
            cols = slice(i * 128, i * 128 + 128)
            return bias_x[:, cols] if row == 4 else conv_x[row : row + 1, cols]
        k = i - 4
        if row == 4:
            pair = [t_bias[e, k : k + 1, :] for e in range(2)]
        else:
            pair = [t_conv[e, row, k : k + 1, :] for e in range(2)]
        return jnp.concatenate(pair, axis=1)

    act_sends = []
    for i in (4, 0, 1, 2, 3, 5):
        cols = slice(i * 128, i * 128 + 128)
        v = ext[:, cols].astype(F32)
        total = jnp.zeros((LEN, 128), F32) + taps_for(i, 4)
        for j in range(4):
            lagged = v if j == 0 else pltpu.roll(v, j, 0)
            total = total + taps_for(i, j) * lagged[16:] * masks[j]
        act[s, :, cols] = (total * lax.logistic(total)).astype(BF16)
        if i < 5:
            tile = act.at[s, :, pl.ds(i * 128, 128)]
            act_sends.append(go(remote(tile, tile, act_s.at[i], act_r.at[i], seq=other)))
    for i in range(2):
        cols = slice(i * 256, i * 256 + 256)
        gate[:, cols] = jnp.dot(stream(), w_zx[:, cols], preferred_element_type=F32).astype(BF16)

    ri = lax.broadcasted_iota(jnp.int32, (LEN, LEN), 0)
    ci = lax.broadcasted_iota(jnp.int32, (LEN, LEN), 1)
    upper = (ri <= ci).astype(F32)
    head_of = lax.broadcasted_iota(jnp.int32, (8, CHAN), 1) // 64
    spread = (head_of == lax.broadcasted_iota(jnp.int32, (8, CHAN), 0)).astype(F32)

    def cumulate(dt):
        return jnp.dot(-rate * dt, upper, precision=HIGH, preferred_element_type=F32)

    def widen(rows):
        return lax.dot_general(rows, spread, TN, precision=HIGH, preferred_element_type=F32)

    dt_own = steps[s]
    cum_r = cumulate(dt_own)
    cum_c = cum_r.T
    seg_r = segment_of(bounds, ci + base)
    seg_c = segment_of(bounds, ri + base)
    valid = (seg_r == seg_c) & (ri >= ci)
    b_own = act[s, :, CHAN : CHAN + STATES]
    c_own = act[s, :, CHAN + STATES :]
    scores = lax.dot_general(c_own, b_own, NT, preferred_element_type=F32)
    scores = jnp.where(valid, scores, 0.0)
    lane = lax.broadcasted_iota(jnp.int32, (LEN, 128), 1)
    for g in range(4):
        cols = slice(g * 128, g * 128 + 128)
        x_pair = act[s, :, cols]
        halves = []
        for h in (2 * g, 2 * g + 1):
            gap = cum_c[:, h : h + 1] - cum_r[h : h + 1, :]
            mix = jnp.exp(jnp.where(valid, gap, 0.0)) * scores * dt_own[h : h + 1, :]
            halves.append(jnp.dot(mix.astype(BF16), x_pair, preferred_element_type=F32))
        acc[:, cols] = jnp.where(lane < 64, halves[0], halves[1])

    step_send.wait_recv()
    for sent in act_sends:
        sent.wait_recv()
    dt_0 = steps[0]
    cum_0 = cumulate(dt_0)
    seg_before = segment_of(bounds, jnp.full((8, LEN), LEN - 1, jnp.int32))
    place = lax.broadcasted_iota(jnp.int32, (8, LEN), 1)
    seg_0 = segment_of(bounds, place)
    seg_1 = segment_of(bounds, place + LEN)
    seg_own = segment_of(bounds, place + base)
    last_0 = cum_0[:, LEN - 1 :]
    into = jnp.exp(last_0 - cum_0) * dt_0 * (seg_0 == seg_before).astype(F32)
    x_0 = act[0, :, :CHAN].astype(F32)
    x_in = (x_0 * widen(into)).astype(BF16)
    entry = lax.dot_general(
        act[0, :, CHAN : CHAN + STATES], x_in, TN, preferred_element_type=F32
    ).astype(BF16)
    carried = ((seg_own == seg_before) & (s > 0)).astype(F32)
    gain = widen(jnp.exp(cum_r) * carried)
    y_all = acc[:, :CHAN] + jnp.dot(c_own, entry, preferred_element_type=F32) * gain
    y_all = y_all + by_head(skip_in, head_of[:1]) * act[s, :, :CHAN].astype(F32)
    gate_f = gate[...].astype(F32)
    gate[...] = (y_all * (gate_f * lax.logistic(gate_f))).astype(BF16)
    out_load.wait()

    def part(zz, yy, cc):
        return pl.ds(pl.multiple_of(zz * 64 + yy * 32 + cc * 16, 16), 16)

    a_copy = []
    b_copy = []

    def to_pal(q):
        cols = slice(q * 1024, q * 1024 + 1024)
        a_copy[q].wait_recv()
        for zz in range(4):
            send_b[q, zz] = (
                acc[part(zz, oy, c), cols] + recv_a[q, zz, oy].astype(F32)
            ).astype(BF16)
        b_copy.append(
            go(remote(send_b.at[q], recv_b.at[q], rsb_s.at[q], rsb_r.at[q], tensor=ypal))
        )
        for zz in range(4):
            keep[q, zz] = acc[part(zz, y, c), cols] + recv_a[q, zz, y].astype(F32)

    for q in range(4):
        for e in range(2):
            cols = slice(q * 1024 + e * 512, q * 1024 + e * 512 + 512)
            acc[:, cols] = jnp.dot(gate[...], w_out[:, cols], preferred_element_type=F32)
        cols = slice(q * 1024, q * 1024 + 1024)
        for zz in range(4):
            for yy in range(2):
                send_a[q, zz, yy] = acc[part(zz, yy, oc), cols].astype(BF16)
        a_copy.append(
            go(remote(send_a.at[q], recv_a.at[q], rsa_s.at[q], rsa_r.at[q], tensor=sib))
        )
        if q > 0:
            to_pal(q - 1)
    to_pal(3)

    def finals_ready():
        dt_1 = steps[1]
        cum_1 = cumulate(dt_1) + last_0
        ends_0 = jnp.zeros((8, LEN), F32)
        ends_1 = jnp.zeros((8, LEN), F32)
        for k in range(n_seg):
            spot_0 = (place == bounds[k] - 1).astype(F32) * cum_0
            spot_1 = (place + LEN == bounds[k] - 1).astype(F32) * cum_1
            end = jnp.sum(spot_0 + spot_1, axis=1, keepdims=True)
            ends_0 = jnp.where(seg_0 == k, end, ends_0)
            ends_1 = jnp.where(seg_1 == k, end, ends_1)
        w_0 = widen(jnp.exp(ends_0 - cum_0) * dt_0)
        w_1 = widen(jnp.exp(ends_1 - cum_1) * dt_1)
        x_1 = act[1, :, :CHAN].astype(F32)
        xw_0 = (x_0 * w_0).astype(BF16)
        xw_1 = (x_1 * w_1).astype(BF16)
        b_0 = act[0, :, CHAN : CHAN + STATES]
        b_1 = act[1, :, CHAN : CHAN + STATES]
        spot = lax.broadcasted_iota(jnp.int32, (LEN, STATES), 0)
        col_0 = segment_of(bounds, spot)
        col_1 = segment_of(bounds, spot + LEN)

        def fill(k):
            m_0 = jnp.where(col_0 == k, b_0.astype(F32), 0.0).astype(BF16)
            m_1 = jnp.where(col_1 == k, b_1.astype(F32), 0.0).astype(BF16)
            fin[k] = lax.dot_general(
                xw_0, m_0, TN, preferred_element_type=F32
            ) + lax.dot_general(xw_1, m_1, TN, preferred_element_type=F32)

        return fill

    c_copy = []
    fill = None
    for q in range(4):
        b_copy[q].wait_recv()
        for d in (2, 1, 3):
            zz = (z + d) % 4
            k = q * 4 + d
            send_c[k] = (keep[q, zz] + recv_b[q, zz].astype(F32)).astype(BF16)
            c_copy.append(
                go(remote(send_c.at[k], recv_c.at[k], rsc_s.at[k], rsc_r.at[k], tensor=zpal[d]))
            )
        if q == 0:
            fill = finals_ready()
        elif q < 3:
            for k in range(n_seg):
                if k % 2 == q - 1:
                    fill(k)
    fin_out = pltpu.make_async_copy(fin, finals, load_sem.at[4])
    fin_out.start()
    for q in range(4):
        total = keep[q, z] + recv_b[q, z].astype(F32)
        for i, d in enumerate((2, 1, 3)):
            c_copy[q * 3 + i].wait_recv()
            total = total + recv_c[q * 4 + d].astype(F32)
        mixed[:, q * 1024 : q * 1024 + 1024] = total.astype(BF16)
    for condition, copy in guarded:
        pl.when(condition)(copy.wait_send)
    for copy in started:
        copy.wait_send()
    fin_out.wait()


def fused_body(
    tokens,
    lengths,
    proj_zx,
    proj_bc,
    proj_dt,
    conv_x,
    conv_bc,
    bias_x,
    bias_bc,
    dt_bias,
    decay_rate,
    skip_gain,
    proj_out,
):
    n_seg = lengths.shape[0]
    bc_view = proj_bc.transpose(1, 2, 0)
    dt_view = proj_dt.T
    any_spec = pl.BlockSpec(memory_space=pl.ANY)
    vmem = pl.BlockSpec(memory_space=pltpu.VMEM)
    smem = pl.BlockSpec(memory_space=pltpu.SMEM)
    dma = pltpu.SemaphoreType.DMA
    mixed, finals = pl.pallas_call(
        layer_kernel,
        out_shape=(
            jax.ShapeDtypeStruct((ROWS, WIDE), BF16),
            jax.ShapeDtypeStruct((n_seg, CHAN, STATES), F32),
        ),
        in_specs=[smem, any_spec, any_spec, any_spec, vmem, vmem, vmem]
        + [any_spec, any_spec, smem, smem, smem, any_spec],
        out_specs=(vmem, any_spec),
        scratch_shapes=[
            pltpu.VMEM((4, 2, 2, ROWS, WIDE), BF16),
            pltpu.VMEM((WIDE, 2, CHAN), BF16),
            pltpu.VMEM((WIDE, 2 * CHAN), BF16),
            pltpu.VMEM((2, 2, 64, WIDE), BF16),
            pltpu.VMEM((CHAN, WIDE), BF16),
            pltpu.VMEM((2, 4, 2, 64), F32),
            pltpu.VMEM((2, 2, 64), F32),
            pltpu.VMEM((LEN, CHAN), BF16),
            pltpu.VMEM((16 + LEN, CHAN + 256), BF16),
            pltpu.VMEM((2, LEN, CHAN + 256), BF16),
            pltpu.VMEM((2, 8, LEN), F32),
            pltpu.VMEM((n_seg, CHAN, STATES), F32),
            pltpu.VMEM((LEN, WIDE), F32),
            pltpu.VMEM((4, 4, ROWS, WIDE // 4), F32),
            pltpu.VMEM((4, 4, 2, ROWS, WIDE // 4), BF16),
            pltpu.VMEM((4, 4, 2, ROWS, WIDE // 4), BF16),
            pltpu.VMEM((4, 4, ROWS, WIDE // 4), BF16),
            pltpu.VMEM((4, 4, ROWS, WIDE // 4), BF16),
            pltpu.VMEM((16, ROWS, WIDE // 4), BF16),
            pltpu.VMEM((16, ROWS, WIDE // 4), BF16),
        ]
        + [dma((k,)) for k in (6, 4, 4, 4, 4, 4, 4, 4, 8, 8, 6, 6, 5, 5)]
        + [dma((k,)) for k in (4, 4, 4, 4, 16, 16)],
        compiler_params=pltpu.CompilerParams(
            collective_id=0, has_side_effects=True, vmem_limit_bytes=60 << 20
        ),
    )(
        lengths,
        tokens,
        proj_zx,
        bc_view,
        dt_view,
        conv_x,
        bias_x.reshape(1, CHAN),
        conv_bc,
        bias_bc,
        dt_bias,
        decay_rate,
        skip_gain,
        proj_out,
    )
    return (mixed, finals.reshape(n_seg, 8, 64, STATES))


def solution(mesh):
    in_specs = (
        P(("seq", "tensor"), None),
        P(),
        P(None, None, "tensor"),
        P(None, None, "tensor"),
        P(None, "tensor"),
        P(None, "tensor"),
        P(None, None, "tensor"),
        P("tensor"),
        P(None, "tensor"),
        P("tensor"),
        P("tensor"),
        P("tensor"),
        P("tensor", None),
    )
    out_specs = (P(("seq", "tensor"), None), P(None, "tensor", None, None))
    small = mesh.shape["seq"] == 2 and mesh.shape["tensor"] == 16
    chosen = fused_body if small else body
    return jax.shard_map(chosen, mesh=mesh, in_specs=in_specs, out_specs=out_specs, check_vma=False)
```
